32 devices in a mesh: gx: 8 (over y, x, core), yz: 4 (over z).
Axes of the slice: x: 2, y: 2, z: 4, core: 2. Of those that a mesh axis runs over, the one named last changes fastest.
Arguments:
- residual: float32 [96, 8, 64, 128], P('gx', 'yz'), may hold values from -0.3 to 0.3
- inverses: float32 [96, 8, 64, 64], P('gx', 'yz'), may hold values from -0.25 to 1
- upwind: float32 [8, 64, 64], replicated, may hold values from -0.25 to 1
- downwind: float32 [8, 64, 64], replicated, may hold values from -0.25 to 1
- flux_y: float32 [8, 64, 64], replicated, may hold values from -0.75 to 0.75
- kinds: int32 [8], P('yz'), may hold values from 0 to 7
- volume_category: int32 [96, 8, 128], P('gx', 'yz'), may hold values from 0 to 2, as said below
Outputs:
- adjoint: float32 [96, 8, 64, 128], P('gx', 'yz')
The draws below stay inside these ranges and needn't reach their ends.
Inputs may be any that keep to these rules, and one draw needn't show every extreme that they name: `volume_category`: 0 marks a fluid cell, 1 a wall cell, 2 an inflow cell.
All inputs are finite; a program needn't handle non-finite values.
Results may differ from the reference program's by a relative error of at most 0.00026.
Values sent between devices are 32-bit elements; how exact they have to be, the bound alone decides.
A program may use at most 64 MiB of HBM per device.

```python
import math
import jax
import jax.numpy as jnp
from jax import lax

NV = 64
NK = 8
NZ = 128
CELLS_PER_XLINE = 96
LINE_GROUP_TOTAL = 8


def rotation(key, lead, strength):
    noise = jax.random.normal(key, lead + (NV, NV), jnp.float32)
    skew_part = strength * 0.5 * (noise - jnp.swapaxes(noise, -1, -2))
    identity = jnp.broadcast_to(jnp.eye(NV, dtype=jnp.float32), lead + (NV, NV))
    term = identity
    total = identity
    for order in range(1, 11):
        term = jnp.matmul(term, skew_part, precision=lax.Precision.HIGHEST) / float(order)
        total = total + term
    return total


def draw_inverses(key, part):
    key_seed_root, key_jagged_draw, key_pulse_draw, key_blend_draw = jax.random.split(key, 4)
    magnitude_multipliers = jnp.exp(jax.random.uniform(key_seed_root, (1, LINE_GROUP_TOTAL, NV, 1), jnp.float32, math.log(0.993), math.log(0.999)))
    irregular_profile = jax.random.uniform(key_jagged_draw, (CELLS_PER_XLINE, LINE_GROUP_TOTAL, NV, 1), jnp.float32, 0.996, 1.0)
    selected_items = jax.random.randint(key_pulse_draw, (CELLS_PER_XLINE, LINE_GROUP_TOTAL, 1, 1), 0, 256)
    sudden_impulses = jnp.where(selected_items == 0, 0.85, 1.0).astype(jnp.float32)

    def one_plane(index):
        return rotation(jax.random.fold_in(key_blend_draw, index), (LINE_GROUP_TOTAL,), 0.04)
    mixing_weights = lax.map(one_plane, jnp.arange(CELLS_PER_XLINE, dtype=jnp.int32))
    return magnitude_multipliers * irregular_profile * sudden_impulses * mixing_weights


def transport_table(key, salt):
    key_scale, key_blend_draw = jax.random.split(jax.random.fold_in(key, salt))
    magnitude_multipliers = jax.random.uniform(key_scale, (NK, NV, 1), jnp.float32, 0.997, 1.0)
    return magnitude_multipliers * rotation(key_blend_draw, (NK,), 0.04)


def draw_upwind(key, part):
    return transport_table(key, 11)


def draw_downwind(key, part):
    return transport_table(key, 23)


def draw_volume_category(key, part):
    selected_items = jax.random.randint(key, (CELLS_PER_XLINE, LINE_GROUP_TOTAL, NZ), 0, 8)
    return jnp.where(selected_items == 0, 1, jnp.where(selected_items == 1, 2, 0)).astype(jnp.int32)


def plant(entries, key, least, high):
    spot = [jax.random.randint(jax.random.fold_in(key, axis), (), 0, length) for axis, length in enumerate(entries.shape)]
    longest = entries.shape.index(max(entries.shape))
    next_to = spot[:longest] + [(spot[longest] + 1) % entries.shape[longest]] + spot[longest + 1:]
    return entries.at[tuple(spot)].set(least).at[tuple(next_to)].set(high)


def block_scale(own_key, extent, shards, least, top_value):
    factor_of = 1.0
    for axis_at, shards_of in shards:
        draws = jax.random.uniform(jax.random.fold_in(jax.random.fold_in(own_key, 6), axis_at), (shards_of,), jnp.float32, least / len(shards), top_value / len(shards))
        factor_of = factor_of * jnp.repeat(jnp.exp(draws), extent[axis_at] // shards_of).reshape((-1,) + (1,) * (len(extent) - 1 - axis_at))
    return factor_of


def gaussian(own_key, extent, deviation, bound, pieces=(), kind=jnp.bfloat16):
    drawn = deviation * jax.random.normal(own_key, extent, jnp.float32)
    if pieces:
        drawn = drawn * block_scale(own_key, extent, pieces, -0.22, 0.18)
    return jnp.clip(drawn, -bound, bound).astype(kind)


def setup_inputs(seed: int = 0) -> dict:
    key_list = jax.random.split(jax.random.key(seed), 8)
    residual = gaussian(key_list[0], (CELLS_PER_XLINE, LINE_GROUP_TOTAL, NV, NZ), 0.05, 0.3, ((0, 8), (1, 4)), jnp.float32)
    inverses = draw_inverses(jax.random.fold_in(key_list[7], 71), 0)
    upwind = draw_upwind(jax.random.fold_in(key_list[7], 71), 0)
    downwind = draw_downwind(jax.random.fold_in(key_list[7], 71), 0)
    flux_y = gaussian(key_list[4], (NK, NV, NV), NV ** -0.5, 0.75, (), jnp.float32)
    kinds = plant(jax.random.randint(key_list[5], (LINE_GROUP_TOTAL,), 0, NK), jax.random.fold_in(key_list[5], 1), 0, NK - 1).astype(jnp.int32)
    volume_category = draw_volume_category(jax.random.fold_in(key_list[7], 71), 0)
    return dict(residual=residual, inverses=inverses, upwind=upwind, downwind=downwind, flux_y=flux_y, kinds=kinds, volume_category=volume_category)


HIGHEST = lax.Precision.HIGHEST


def apply_transposed(matrices, vectors):
    return jnp.einsum("gab,gaz->gbz", matrices, vectors, precision=HIGHEST)


def select_rows(kinds, table):
    kind_count = table.shape[0]
    one_hot = (kinds[:, None] == jnp.arange(kind_count, dtype=jnp.int32)[None, :]).astype(jnp.float32)
    flat = jnp.dot(one_hot, table.reshape(kind_count, -1), precision=HIGHEST, preferred_element_type=jnp.float32)
    return flat.reshape(kinds.shape[0], table.shape[1], table.shape[2])


def source_weight(volume_category):
    fluid = (volume_category == 0).astype(jnp.float32)
    inflow = (volume_category == 2).astype(jnp.float32)
    return (fluid + 0.5 * inflow)[:, :, None, :]


def y_derivative(padded):
    return (8.0 * (padded[:, 3:-1] - padded[:, 1:-3]) - (padded[:, 4:] - padded[:, :-4])) / 12.0


def reference(residual, inverses, upwind, downwind, flux_y, kinds, volume_category):
    up_rows = select_rows(kinds, upwind)
    lower_neighbors = select_rows(kinds, downwind)
    flux_rows = select_rows(kinds, flux_y)
    padded = jnp.pad(residual, ((0, 0), (2, 2), (0, 0), (0, 0)))
    derivative = y_derivative(padded)
    flux = jnp.einsum("yab,xyaz->xybz", flux_rows, derivative, precision=HIGHEST)
    forcing = source_weight(volume_category) * (residual + flux)

    def forward_step(carried, cell_data):
        forcing_cell, inverse_cell = cell_data
        eliminated = forcing_cell - apply_transposed(up_rows, carried)
        return apply_transposed(inverse_cell, eliminated), eliminated

    initial = jnp.zeros((residual.shape[1], residual.shape[2], residual.shape[3]), jnp.float32)
    last_value, eliminated = lax.scan(forward_step, initial, (forcing, inverses))

    def backward_step(carried, cell_data):
        eliminated_cell, inverse_cell = cell_data
        updated = apply_transposed(inverse_cell, eliminated_cell - apply_transposed(lower_neighbors, carried))
        return updated, updated

    first_value, adjoint = lax.scan(backward_step, initial, (eliminated, inverses), reverse=True)
    wet_cells = (volume_category != 1).astype(jnp.float32)[:, :, None, :]
    return adjoint * wet_cells
```

```python
import functools

import jax
import jax.numpy as jnp
from jax import lax
from jax.experimental import pallas as pl
from jax.experimental.pallas import tpu as pltpu
from jax.sharding import PartitionSpec as P

MESH = pl.DeviceIdType.MESH
F32 = jnp.float32
BF16 = jnp.bfloat16


def split(a):
    high = a.astype(BF16)
    return high, (a - high.astype(F32)).astype(BF16)


def mul(a, b):
    ah, al = a
    bh, bl = b
    d = functools.partial(jnp.dot, preferred_element_type=F32)
    return d(ah, bh) + (d(ah, bl) + d(al, bh))


def kernel(
    n_gx, n_yz, chunk, kinds, res, inv, up, down, flux, cat, out,
    snd, low, high, table, vt, ft, bt, hom, resp, cs, gmap, gvec, cin, into,
    halo_send, halo_recv, map_send, map_recv, vec_send, vec_recv,
):
    cells, groups, nv, nz = res.shape
    gx = lax.axis_index("gx")
    yz = lax.axis_index("yz")
    has_low = yz > 0
    has_high = yz < n_yz - 1

    barrier = pltpu.get_barrier_semaphore()
    for k in range(1, n_gx):
        pl.semaphore_signal(
            barrier, inc=1, device_id=(lax.rem(gx + k, n_gx), yz), device_id_type=MESH
        )

    @pl.when(has_low)
    def _():
        pl.semaphore_signal(barrier, inc=1, device_id=(gx, yz - 1), device_id_type=MESH)

    @pl.when(has_high)
    def _():
        pl.semaphore_signal(barrier, inc=1, device_id=(gx, yz + 1), device_id_type=MESH)

    def combos(x, carry):
        first, second = res[x, 0], res[x, 1]
        snd[0, x] = first - 8.0 * second
        snd[1, x] = 8.0 * first - second
        return carry

    lax.fori_loop(0, cells, combos, 0)

    pl.semaphore_wait(
        barrier, n_gx - 1 + jnp.where(has_low, 1, 0) + jnp.where(has_high, 1, 0)
    )

    pieces = cells // chunk

    def halo(direction, g, c):
        part = pl.ds(c * chunk, chunk)
        if direction == 0:
            src = snd.at[0, part] if g == 0 else res.at[part, 1]
            dst, where = low, yz + 1
        else:
            src = res.at[part, 0] if g == 0 else snd.at[1, part]
            dst, where = high, yz - 1
        return pltpu.make_async_remote_copy(
            src_ref=src,
            dst_ref=dst.at[g, part],
            send_sem=halo_send.at[direction, g, c],
            recv_sem=halo_recv.at[direction, g, c],
            device_id=(gx, where),
            device_id_type=MESH,
        )

    @pl.when(has_high)
    def _():
        for g in range(groups):
            for c in range(pieces):
                halo(0, g, c).start()

    @pl.when(has_low)
    def _():
        for g in range(groups):
            for c in range(pieces):
                halo(1, g, c).start()

    @pl.when(jnp.logical_not(has_low))
    def _():
        low[...] = jnp.zeros_like(low)

    @pl.when(jnp.logical_not(has_high))
    def _():
        high[...] = jnp.zeros_like(high)

    for g in range(groups):
        kind = kinds[g]
        for n, block in enumerate((flux[kind] * (1.0 / 12.0), -up[kind], -down[kind])):
            table[g, n, 0], table[g, n, 1] = split(block.T)

    def held(g, n):
        return table[g, n, 0], table[g, n, 1]

    def put(ref, g, x, pair):
        ref[g, x, 0], ref[g, x, 1] = pair

    def get(ref, g, x):
        return ref[g, x, 0], ref[g, x, 1]

    def steps(x, carry):
        for g in range(groups):
            v = split(inv[x, g].T)
            put(vt, g, x, v)
            put(ft, g, x, split(mul(v, held(g, 1))))
            put(bt, g, x, split(mul(v, held(g, 2))))
        return carry

    lax.fori_loop(0, cells, steps, 0)

    row = lax.broadcasted_iota(jnp.int32, (nv, 2 * nv), 0)
    col = lax.broadcasted_iota(jnp.int32, (nv, 2 * nv), 1)
    first_unit = (row == col).astype(F32)
    second_unit = (row + nv == col).astype(F32)

    for g in range(groups):
        hom[g, 0] = first_unit

    def hom_forward(x, carry):
        for g in range(groups):
            hom[g, x + 1] = mul(get(ft, g, x), split(hom[g, x]))
        return carry

    lax.fori_loop(0, cells, hom_forward, 0)

    def hom_backward(i, state):
        x = cells - 1 - i
        new = []
        for g in range(groups):
            m = hom[g, x + 1] + mul(get(bt, g, x), split(state[g]))
            put(resp, g, x, split(m))
            new.append(m)
        return tuple(new)

    firsts = lax.fori_loop(0, cells, hom_backward, (second_unit,) * groups)
    for g in range(groups):
        gmap[gx, g, :nv] = hom[g, cells]
        gmap[gx, g, nv:] = firsts[g]

    def share_map(k):
        return pltpu.make_async_remote_copy(
            src_ref=gmap.at[gx],
            dst_ref=gmap.at[gx],
            send_sem=map_send.at[k],
            recv_sem=map_recv.at[gx],
            device_id=(lax.rem(gx + k, n_gx), yz),
            device_id_type=MESH,
        )

    def take_map(k):
        source = lax.rem(gx + k, n_gx)
        return pltpu.make_async_remote_copy(
            src_ref=gmap.at[source],
            dst_ref=gmap.at[source],
            send_sem=map_send.at[k],
            recv_sem=map_recv.at[source],
            device_id=(source, yz),
            device_id_type=MESH,
        )

    def share_vec(g, k):
        return pltpu.make_async_remote_copy(
            src_ref=gvec.at[g, gx],
            dst_ref=gvec.at[g, gx],
            send_sem=vec_send.at[g, k],
            recv_sem=vec_recv.at[g, gx],
            device_id=(lax.rem(gx + k, n_gx), yz),
            device_id_type=MESH,
        )

    def take_vec(g, k):
        source = lax.rem(gx + k, n_gx)
        return pltpu.make_async_remote_copy(
            src_ref=gvec.at[g, source],
            dst_ref=gvec.at[g, source],
            send_sem=vec_send.at[g, k],
            recv_sem=vec_recv.at[g, source],
            device_id=(source, yz),
            device_id_type=MESH,
        )

    for k in range(1, n_gx):
        share_map(k).start()

    for g in range(groups):
        c_state = jnp.zeros((nv, nz), F32)
        for c in range(pieces):
            @pl.when(has_low)
            def _():
                halo(0, g, c).wait_recv()

            @pl.when(has_high)
            def _():
                halo(1, g, c).wait_recv()

            def forward(x, state):
                if g == 0:
                    derivative = 8.0 * res[x, 1] + low[g, x] - high[g, x]
                else:
                    derivative = low[g, x] + high[g, x] - 8.0 * res[x, 0]
                kind = cat[x][g : g + 1]
                weight = jnp.where(kind == 0, 1.0, jnp.where(kind == 2, 0.5, 0.0))
                force = weight * (res[x, g] + mul(held(g, 0), split(derivative)))
                state = mul(get(vt, g, x), split(force)) + mul(get(ft, g, x), split(state))
                cs[g, x] = state
                return state

            c_state = lax.fori_loop(c * chunk, (c + 1) * chunk, forward, c_state)

        def backward(i, state):
            x = cells - 1 - i
            state = cs[g, x] + mul(get(bt, g, x), split(state))
            cs[g, x] = state
            return state

        l_state = lax.fori_loop(0, cells, backward, jnp.zeros((nv, nz), F32))
        gvec[g, gx, :nv] = c_state
        gvec[g, gx, nv:] = l_state
        for k in range(1, n_gx):
            share_vec(g, k).start()

    for k in range(1, n_gx):
        take_map(k).wait_recv()

    for g in range(groups):
        for k in range(1, n_gx):
            take_vec(g, k).wait_recv()

        def ahead(j, state):
            cin[g, j, :nv] = state
            return gvec[g, j, :nv] + mul(split(gmap[j, g, :nv, :nv]), split(state))

        lax.fori_loop(0, n_gx, ahead, jnp.zeros((nv, nz), F32))

        def behind(i, state):
            j = n_gx - 1 - i
            cin[g, j, nv:] = state
            return gvec[g, j, nv:] + mul(split(gmap[j, g, nv:]), split(cin[g, j]))

        def behind_step(i, state):
            return behind(i, state)

        lax.fori_loop(0, n_gx, behind_step, jnp.zeros((nv, nz), F32))
        into[g, 0], into[g, 1] = split(cin[g, gx])

        def finish(x, carry):
            out[x, g] = cs[g, x] + mul(get(resp, g, x), (into[g, 0], into[g, 1]))
            return carry

        lax.fori_loop(0, cells, finish, 0)

    @pl.when(has_high)
    def _():
        for g in range(groups):
            for c in range(pieces):
                halo(0, g, c).wait_send()

    @pl.when(has_low)
    def _():
        for g in range(groups):
            for c in range(pieces):
                halo(1, g, c).wait_send()

    for k in range(1, n_gx):
        share_map(k).wait_send()
        for g in range(groups):
            share_vec(g, k).wait_send()


def per_device(n_gx, n_yz, residual, inverses, upwind, downwind, flux_y, kinds, volume_category):
    cells, groups, nv, nz = residual.shape
    chunk = next(c for c in (3, 4, 2, 1) if cells % c == 0)
    pieces = cells // chunk
    vmem = pl.BlockSpec(memory_space=pltpu.VMEM)
    swept = pl.pallas_call(
        functools.partial(kernel, n_gx, n_yz, chunk),
        out_shape=jax.ShapeDtypeStruct(residual.shape, F32),
        in_specs=[pl.BlockSpec(memory_space=pltpu.SMEM)] + [vmem] * 6,
        out_specs=vmem,
        scratch_shapes=[
            pltpu.VMEM((2, cells, nv, nz), F32),
            pltpu.VMEM((groups, cells, nv, nz), F32),
            pltpu.VMEM((groups, cells, nv, nz), F32),
            pltpu.VMEM((groups, 3, 2, nv, nv), BF16),
            pltpu.VMEM((groups, cells, 2, nv, nv), BF16),
            pltpu.VMEM((groups, cells, 2, nv, nv), BF16),
            pltpu.VMEM((groups, cells, 2, nv, nv), BF16),
            pltpu.VMEM((groups, cells + 1, nv, 2 * nv), F32),
            pltpu.VMEM((groups, cells, 2, nv, 2 * nv), BF16),
            pltpu.VMEM((groups, cells, nv, nz), F32),
            pltpu.VMEM((n_gx, groups, 2 * nv, 2 * nv), F32),
            pltpu.VMEM((groups, n_gx, 2 * nv, nz), F32),
            pltpu.VMEM((groups, n_gx, 2 * nv, nz), F32),
            pltpu.VMEM((groups, 2, 2 * nv, nz), BF16),
            pltpu.SemaphoreType.DMA((2, groups, pieces)),
            pltpu.SemaphoreType.DMA((2, groups, pieces)),
            pltpu.SemaphoreType.DMA((n_gx,)),
            pltpu.SemaphoreType.DMA((n_gx,)),
            pltpu.SemaphoreType.DMA((groups, n_gx)),
            pltpu.SemaphoreType.DMA((groups, n_gx)),
        ],
        compiler_params=pltpu.CompilerParams(
            collective_id=0, has_side_effects=True, vmem_limit_bytes=48 * 1024 * 1024
        ),
    )(kinds, residual, inverses, upwind, downwind, flux_y, volume_category)
    return jnp.where((volume_category != 1)[:, :, None, :], swept, 0.0)


def solution(mesh):
    in_specs = (
        P("gx", "yz", None, None),
        P("gx", "yz", None, None),
        P(),
        P(),
        P(),
        P("yz"),
        P("gx", "yz", None),
    )
    out_specs = P("gx", "yz", None, None)
    return jax.shard_map(
        functools.partial(per_device, mesh.shape["gx"], mesh.shape["yz"]),
        mesh=mesh,
        in_specs=in_specs,
        out_specs=out_specs,
        check_vma=False,
    )
```

```python
import functools

import jax
import jax.numpy as jnp
from jax import lax
from jax.experimental import pallas as pl
from jax.experimental.pallas import tpu as pltpu
from jax.sharding import PartitionSpec as P

MESH = pl.DeviceIdType.MESH
F32 = jnp.float32
BF16 = jnp.bfloat16


def split(a):
    high = a.astype(BF16)
    return high, (a - high.astype(F32)).astype(BF16)


def mul(a, b):
    ah, al = a
    bh, bl = b
    d = functools.partial(jnp.dot, preferred_element_type=F32)
    return d(ah, bh) + (d(ah, bl) + d(al, bh))


def loop(count, body, carry, unroll=1):
    unroll = unroll if count % unroll == 0 else 1

    def several(i, carry):
        for u in range(unroll):
            carry = body(i * unroll + u, carry)
        return carry

    return lax.fori_loop(0, count // unroll, several, carry)


def kernel(
    n_gx, n_yz, chunk, kinds, res_hbm, inv_hbm, up_hbm, down_hbm, flux_hbm, cat_hbm, out,
    res, inv, up, down, flux, cat,
    snd, low, high, table, vt, ft, bt, hom, omega, lam, resp, cs, gmap, gvec, wc, wl, into, side, wide_state, tall,
    load_sem, halo_send, halo_recv, map_send, map_recv, vec_send, vec_recv,
):
    cells, groups, nv, nz = res.shape
    half = n_gx // 2
    pieces = cells // chunk
    gx = lax.axis_index("gx")
    yz = lax.axis_index("yz")
    partner = gx + 1 - 2 * lax.rem(gx, 2)
    has_low = yz > 0
    has_high = yz < n_yz - 1

    loads = [
        pltpu.make_async_copy(source, target, load_sem.at[n])
        for n, (source, target) in enumerate(
            (
                (res_hbm, res), (inv_hbm, inv), (up_hbm, up), (down_hbm, down),
                (flux_hbm, flux), (cat_hbm, cat),
            )
        )
    ]
    for load in loads:
        load.start()

    def peer(k):
        return lax.rem(gx + 2 * k, n_gx)

    barrier = pltpu.get_barrier_semaphore()
    for k in range(1, half):
        pl.semaphore_signal(barrier, inc=1, device_id=(peer(k), yz), device_id_type=MESH)
    pl.semaphore_signal(barrier, inc=1, device_id=(partner, yz), device_id_type=MESH)

    @pl.when(has_low)
    def _():
        pl.semaphore_signal(barrier, inc=1, device_id=(gx, yz - 1), device_id_type=MESH)

    @pl.when(has_high)
    def _():
        pl.semaphore_signal(barrier, inc=1, device_id=(gx, yz + 1), device_id_type=MESH)

    pl.semaphore_wait(barrier, half + jnp.where(has_low, 1, 0) + jnp.where(has_high, 1, 0))

    def halo(direction, g, c):
        part = pl.ds(c * chunk, chunk)
        if direction == 0:
            src = snd.at[0, part] if g == 0 else res_hbm.at[part, 1]
            dst, where = low, yz + 1
        else:
            src = res_hbm.at[part, 0] if g == 0 else snd.at[1, part]
            dst, where = high, yz - 1
        return pltpu.make_async_remote_copy(
            src_ref=src,
            dst_ref=dst.at[g, part],
            send_sem=halo_send.at[direction, g, c],
            recv_sem=halo_recv.at[direction, g, c],
            device_id=(gx, where),
            device_id_type=MESH,
        )

    @pl.when(has_low)
    def _():
        for c in range(pieces):
            halo(1, 0, c).start()

    loads[0].wait()

    for c in range(pieces):
        for x in range(c * chunk, (c + 1) * chunk):
            snd[0, x] = res[x, 0] - 8.0 * res[x, 1]

        @pl.when(has_high)
        def _():
            halo(0, 0, c).start()

    @pl.when(has_high)
    def _():
        for c in range(pieces):
            halo(0, 1, c).start()

    for c in range(pieces):
        for x in range(c * chunk, (c + 1) * chunk):
            snd[1, x] = 8.0 * res[x, 0] - res[x, 1]

        @pl.when(has_low)
        def _():
            halo(1, 1, c).start()

    @pl.when(jnp.logical_not(has_low))
    def _():
        low[...] = jnp.zeros_like(low)

    @pl.when(jnp.logical_not(has_high))
    def _():
        high[...] = jnp.zeros_like(high)

    for load in loads[1:]:
        load.wait()

    for g in range(groups):
        kind = kinds[g]
        for n, block in enumerate((flux[kind] * (1.0 / 12.0), -up[kind], -down[kind])):
            table[g, n, 0], table[g, n, 1] = split(block.T)

    def held(g, n):
        return table[g, n, 0], table[g, n, 1]

    def put(ref, g, x, pair):
        ref[g, x, 0], ref[g, x, 1] = pair

    def get(ref, g, x):
        return ref[g, x, 0], ref[g, x, 1]

    def steps(x, carry):
        for g in range(groups):
            v = split(inv[x, g].T)
            put(vt, g, x, v)
            put(ft, g, x, split(mul(v, held(g, 1))))
            put(bt, g, x, split(mul(v, held(g, 2))))
        return carry

    loop(cells, steps, 0, 4)

    row = lax.broadcasted_iota(jnp.int32, (nv, 2 * nv), 0)
    col = lax.broadcasted_iota(jnp.int32, (nv, 2 * nv), 1)
    first_unit = (row == col).astype(F32)
    second_unit = (row + nv == col).astype(F32)
    square_row = lax.broadcasted_iota(jnp.int32, (nv, nv), 0)
    square_col = lax.broadcasted_iota(jnp.int32, (nv, nv), 1)
    unit = (square_row == square_col).astype(F32)
    for g in range(groups):
        hom[g, 0] = first_unit
        omega[g, 0] = unit

    def hom_forward(x, carry):
        for g in range(groups):
            hom[g, x + 1] = mul(get(ft, g, x), split(hom[g, x]))
            omega[g, x + 1] = mul(split(omega[g, x]), get(bt, g, x))
        return carry

    loop(cells, hom_forward, 0)

    for g in range(groups):
        side[g] = jnp.zeros((nv, nv), F32)
        wide_state[g] = second_unit

    def hom_backward(i, carry):
        x = cells - 1 - i
        for g in range(groups):
            m = hom[g, x + 1] + mul(get(bt, g, x), split(wide_state[g]))
            put(resp, g, x, split(m))
            wide_state[g] = m
            now = split(omega[g, x] + side[g])
            put(lam, g, x, now)
            side[g] = mul(now, get(ft, g, x))
        return carry

    loop(cells, hom_backward, 0)
    for g in range(groups):
        gmap[gx, g * nv : (g + 1) * nv] = wide_state[g]
    gmap[gx, groups * nv :] = jnp.concatenate(
        [hom[g, cells][:, :nv] for g in range(groups)], axis=1
    )

    def share(buffer, send, recv, slot, target, k):
        return pltpu.make_async_remote_copy(
            src_ref=buffer.at[slot],
            dst_ref=buffer.at[slot],
            send_sem=send.at[k],
            recv_sem=recv.at[slot],
            device_id=(target, yz),
            device_id_type=MESH,
        )

    def offer(*where):
        for k in range(1, half):
            share(*where, gx, peer(k), k).start()
        share(*where, gx, partner, 0).start()

    def relay(*where):
        for k in range(1, half):
            share(*where, peer(k), peer(k), k).wait_recv()
            share(*where, peer(k), partner, half + k).start()

    def collect(*where):
        share(*where, partner, partner, 0).wait_recv()
        for k in range(1, half):
            share(*where, lax.rem(partner + 2 * k, n_gx), partner, half + k).wait_recv()

    def release(*where):
        share(*where, gx, partner, 0).wait_send()
        for k in range(1, half):
            share(*where, gx, peer(k), k).wait_send()
            share(*where, peer(k), partner, half + k).wait_send()

    maps = (gmap, map_send, map_recv)
    vecs = [(gvec.at[g], vec_send.at[g], vec_recv.at[g]) for g in range(groups)]
    offer(*maps)

    def local_forward(g):
        state = (jnp.zeros((nv, nz), F32), jnp.zeros((nv, nz), F32))
        for c in range(pieces):
            @pl.when(has_low)
            def _():
                halo(0, g, c).wait_recv()

            @pl.when(has_high)
            def _():
                halo(1, g, c).wait_recv()

            def forward(i, state):
                x = c * chunk + i
                last, first = state
                if g == 0:
                    derivative = 8.0 * res[x, 1] + low[g, x] - high[g, x]
                else:
                    derivative = low[g, x] + high[g, x] - 8.0 * res[x, 0]
                kind = cat[x][g : g + 1]
                weight = jnp.where(kind == 0, 1.0, jnp.where(kind == 2, 0.5, 0.0))
                force = weight * (res[x, g] + mul(held(g, 0), split(derivative)))
                driven = mul(get(vt, g, x), split(force))
                last = driven + mul(get(ft, g, x), split(last))
                first = first + mul(get(lam, g, x), split(driven))
                cs[g, x] = last
                return last, first

            state = loop(chunk, forward, state, chunk)
        gvec[g, gx, :nv] = state[0]
        gvec[g, gx, nv:] = state[1]

    def local_backward(g):
        def backward(i, state):
            x = cells - 1 - i
            state = cs[g, x] + mul(get(bt, g, x), split(state))
            cs[g, x] = state
            return state

        loop(cells, backward, jnp.zeros((nv, nz), F32))

    def finish(g):
        total = jnp.zeros((2 * nv, nz), F32)
        tail = jnp.zeros((nv, nz), F32)
        for j in range(n_gx):
            total = total + mul(get(wc, g, j), split(gvec[g, j, :nv]))
            tail = tail + mul(get(wl, g, j), split(gvec[g, j, nv:]))
        into[g, 0, :nv], into[g, 1, :nv] = split(total[:nv])
        into[g, 0, nv:], into[g, 1, nv:] = split(total[nv:] + tail)

        def fix(x, carry):
            value = cs[g, x] + mul(get(resp, g, x), (into[g, 0], into[g, 1]))
            out[x, g] = jnp.where(cat[x][g : g + 1] != 1, value, 0.0)
            return carry

        loop(cells, fix, 0, 4)

    local_forward(0)
    offer(*vecs[0])
    relay(*maps)
    local_backward(0)
    collect(*maps)

    for g in range(groups):
        side[g] = jnp.zeros((nv, nv), F32)
        tall[g] = jnp.zeros((2 * nv, nv), F32)

    def suffix(j, carry):
        here = jnp.where(gx == j, 1.0, 0.0)
        for g in range(groups):
            e = split(side[g])
            put(wl, g, j, e)
            both = mul(e, split(gmap[j, g * nv : (g + 1) * nv]))
            side[g] = both[:, nv:] + here * unit
            hom[g, j] = both
        return carry

    loop(n_gx, suffix, 0)

    def prefix(i, carry):
        j = n_gx - 1 - i
        here = jnp.where(gx == j, 1.0, 0.0)
        maps_here = gmap[j, groups * nv :]
        for g in range(groups):
            xs = split(tall[g])
            put(wc, g, j, xs)
            nxt = mul(xs, split(maps_here[:, g * nv : (g + 1) * nv]))
            tall[g, :nv] = nxt[:nv] + here * unit
            tall[g, nv:] = nxt[nv:] + hom[g, j][:, :nv]
        return carry

    loop(n_gx, prefix, 0)

    relay(*vecs[0])
    for g in range(1, groups):
        local_forward(g)
        offer(*vecs[g])
        local_backward(g)
        relay(*vecs[g])
    for g in range(groups):
        collect(*vecs[g])
        finish(g)

    @pl.when(has_high)
    def _():
        for g in range(groups):
            for c in range(pieces):
                halo(0, g, c).wait_send()

    @pl.when(has_low)
    def _():
        for g in range(groups):
            for c in range(pieces):
                halo(1, g, c).wait_send()

    release(*maps)
    for g in range(groups):
        release(*vecs[g])


def per_device(n_gx, n_yz, residual, inverses, upwind, downwind, flux_y, kinds, volume_category):
    cells, groups, nv, nz = residual.shape
    chunk = next(c for c in (3, 4, 2, 1) if cells % c == 0)
    pieces = cells // chunk
    hbm = pl.BlockSpec(memory_space=pltpu.HBM)
    operands = (residual, inverses, upwind, downwind, flux_y, volume_category)
    square = pltpu.VMEM((groups, cells, 2, nv, nv), BF16)
    wide = pltpu.VMEM((groups, cells, nv, nz), F32)
    return pl.pallas_call(
        functools.partial(kernel, n_gx, n_yz, chunk),
        out_shape=jax.ShapeDtypeStruct(residual.shape, F32),
        in_specs=[pl.BlockSpec(memory_space=pltpu.SMEM)] + [hbm] * 6,
        out_specs=pl.BlockSpec(memory_space=pltpu.VMEM),
        scratch_shapes=[pltpu.VMEM(a.shape, a.dtype) for a in operands]
        + [
            pltpu.VMEM((2, cells, nv, nz), F32),
            wide,
            wide,
            pltpu.VMEM((groups, 3, 2, nv, nv), BF16),
            square,
            square,
            square,
            pltpu.VMEM((groups, max(cells, n_gx) + 1, nv, 2 * nv), F32),
            pltpu.VMEM((groups, cells + 1, nv, nv), F32),
            square,
            pltpu.VMEM((groups, cells, 2, nv, 2 * nv), BF16),
            wide,
            pltpu.VMEM((n_gx, (groups + 1) * nv, 2 * nv), F32),
            pltpu.VMEM((groups, n_gx, 2 * nv, nz), F32),
            pltpu.VMEM((groups, n_gx, 2, 2 * nv, nv), BF16),
            pltpu.VMEM((groups, n_gx, 2, nv, nv), BF16),
            pltpu.VMEM((groups, 2, 2 * nv, nz), BF16),
            pltpu.VMEM((groups, nv, nv), F32),
            pltpu.VMEM((groups, nv, 2 * nv), F32),
            pltpu.VMEM((groups, 2 * nv, nv), F32),
            pltpu.SemaphoreType.DMA((6,)),
            pltpu.SemaphoreType.DMA((2, groups, pieces)),
            pltpu.SemaphoreType.DMA((2, groups, pieces)),
            pltpu.SemaphoreType.DMA((n_gx,)),
            pltpu.SemaphoreType.DMA((n_gx,)),
            pltpu.SemaphoreType.DMA((groups, n_gx)),
            pltpu.SemaphoreType.DMA((groups, n_gx)),
        ],
        compiler_params=pltpu.CompilerParams(
            collective_id=0, has_side_effects=True, vmem_limit_bytes=67043328
        ),
    )(kinds, *operands)


def solution(mesh):
    in_specs = (
        P("gx", "yz", None, None),
        P("gx", "yz", None, None),
        P(),
        P(),
        P(),
        P("yz"),
        P("gx", "yz", None),
    )
    out_specs = P("gx", "yz", None, None)
    return jax.shard_map(
        functools.partial(per_device, mesh.shape["gx"], mesh.shape["yz"]),
        mesh=mesh,
        in_specs=in_specs,
        out_specs=out_specs,
        check_vma=False,
    )
```

```python
import functools

import jax
import jax.numpy as jnp
from jax import lax
from jax.experimental import pallas as pl
from jax.experimental.pallas import tpu as pltpu
from jax.sharding import PartitionSpec as P

MESH = pl.DeviceIdType.MESH
F32 = jnp.float32
BF16 = jnp.bfloat16


def split(a):
    high = a.astype(BF16)
    return high, (a - high.astype(F32)).astype(BF16)


def mul(a, b):
    ah, al = a
    bh, bl = b
    d = functools.partial(jnp.dot, preferred_element_type=F32)
    return d(ah, bh) + (d(ah, bl) + d(al, bh))


def loop(count, body, carry, unroll=1):
    unroll = unroll if count % unroll == 0 else 1

    def several(i, carry):
        for u in range(unroll):
            carry = body(i * unroll + u, carry)
        return carry

    return lax.fori_loop(0, count // unroll, several, carry)


def kernel(
    n_gx, n_yz, chunk, res_hbm, inv_hbm, up_hbm, down_hbm, flux_hbm, cat_hbm, kinds_hbm, out,
    res, inv, up, down, flux, cat, kinds,
    snd, low, high, table, vt, ft, bt, hom, omega, lam, resp, cs, gmap, gvec, wc, wl, into, side, wide_state, tall, into_state,
    load_sem, halo_send, halo_recv, map_send, map_recv, vec_send, vec_recv,
):
    cells, groups, nv, nz = res.shape
    half = n_gx // 2
    pieces = cells // chunk
    gx = lax.axis_index("gx")
    yz = lax.axis_index("yz")
    partner = gx + 1 - 2 * lax.rem(gx, 2)
    has_low = yz > 0
    has_high = yz < n_yz - 1

    loads = [
        pltpu.make_async_copy(source, target, load_sem.at[n])
        for n, (source, target) in enumerate(
            (
                (res_hbm, res), (inv_hbm, inv), (up_hbm, up), (down_hbm, down),
                (flux_hbm, flux), (cat_hbm, cat), (kinds_hbm, kinds),
            )
        )
    ]
    for load in loads:
        load.start()

    def peer(k):
        return lax.rem(gx + 2 * k, n_gx)

    barrier = pltpu.get_barrier_semaphore()
    for k in range(1, half):
        pl.semaphore_signal(barrier, inc=1, device_id=(peer(k), yz), device_id_type=MESH)
    pl.semaphore_signal(barrier, inc=1, device_id=(partner, yz), device_id_type=MESH)

    @pl.when(has_low)
    def _():
        pl.semaphore_signal(barrier, inc=1, device_id=(gx, yz - 1), device_id_type=MESH)

    @pl.when(has_high)
    def _():
        pl.semaphore_signal(barrier, inc=1, device_id=(gx, yz + 1), device_id_type=MESH)

    pl.semaphore_wait(barrier, half + jnp.where(has_low, 1, 0) + jnp.where(has_high, 1, 0))

    def halo(direction, g, c):
        part = pl.ds(c * chunk, chunk)
        if direction == 0:
            src = snd.at[0, part] if g == 0 else res_hbm.at[part, 1]
            dst, where = low, yz + 1
        else:
            src = res_hbm.at[part, 0] if g == 0 else snd.at[1, part]
            dst, where = high, yz - 1
        return pltpu.make_async_remote_copy(
            src_ref=src,
            dst_ref=dst.at[g, part],
            send_sem=halo_send.at[direction, g, c],
            recv_sem=halo_recv.at[direction, g, c],
            device_id=(gx, where),
            device_id_type=MESH,
        )

    @pl.when(has_low)
    def _():
        for c in range(pieces):
            halo(1, 0, c).start()

    loads[0].wait()

    for c in range(pieces):
        for x in range(c * chunk, (c + 1) * chunk):
            snd[0, x] = res[x, 0] - 8.0 * res[x, 1]

        @pl.when(has_high)
        def _():
            halo(0, 0, c).start()

    @pl.when(has_high)
    def _():
        for c in range(pieces):
            halo(0, 1, c).start()

    for c in range(pieces):
        for x in range(c * chunk, (c + 1) * chunk):
            snd[1, x] = 8.0 * res[x, 0] - res[x, 1]

        @pl.when(has_low)
        def _():
            halo(1, 1, c).start()

    @pl.when(jnp.logical_not(has_low))
    def _():
        low[...] = jnp.zeros_like(low)

    @pl.when(jnp.logical_not(has_high))
    def _():
        high[...] = jnp.zeros_like(high)

    for load in loads[1:]:
        load.wait()

    for g in range(groups):
        kind = kinds[g]
        for n, block in enumerate((flux[kind] * (1.0 / 12.0), -up[kind], -down[kind])):
            table[g, n, 0], table[g, n, 1] = split(block.T)

    def held(g, n):
        return table[g, n, 0], table[g, n, 1]

    def put(ref, g, x, pair):
        ref[g, x, 0], ref[g, x, 1] = pair

    def get(ref, g, x):
        return ref[g, x, 0], ref[g, x, 1]

    def steps(x, carry):
        for g in range(groups):
            v = split(inv[x, g].T)
            put(vt, g, x, v)
            put(ft, g, x, split(mul(v, held(g, 1))))
            put(bt, g, x, split(mul(v, held(g, 2))))
        return carry

    loop(cells, steps, 0, 4)

    row = lax.broadcasted_iota(jnp.int32, (nv, 2 * nv), 0)
    col = lax.broadcasted_iota(jnp.int32, (nv, 2 * nv), 1)
    first_unit = (row == col).astype(F32)
    second_unit = (row + nv == col).astype(F32)
    square_row = lax.broadcasted_iota(jnp.int32, (nv, nv), 0)
    square_col = lax.broadcasted_iota(jnp.int32, (nv, nv), 1)
    unit = (square_row == square_col).astype(F32)
    for g in range(groups):
        hom[g, 0] = first_unit
        omega[g, 0] = unit

    def hom_forward(x, carry):
        for g in range(groups):
            hom[g, x + 1] = mul(get(ft, g, x), split(hom[g, x]))
            omega[g, x + 1] = mul(split(omega[g, x]), get(bt, g, x))
        return carry

    loop(cells, hom_forward, 0)

    for g in range(groups):
        side[g] = jnp.zeros((nv, nv), F32)
        wide_state[g] = second_unit

    def hom_backward(i, carry):
        x = cells - 1 - i
        for g in range(groups):
            m = hom[g, x + 1] + mul(get(bt, g, x), split(wide_state[g]))
            put(resp, g, x, split(m))
            wide_state[g] = m
            now = split(omega[g, x] + side[g])
            put(lam, g, x, now)
            side[g] = mul(now, get(ft, g, x))
        return carry

    loop(cells, hom_backward, 0)
    for g in range(groups):
        gmap[gx, g * nv : (g + 1) * nv] = wide_state[g]
    gmap[gx, groups * nv :] = jnp.concatenate(
        [hom[g, cells][:, :nv] for g in range(groups)], axis=1
    )

    def share(buffer, send, recv, slot, target, k):
        return pltpu.make_async_remote_copy(
            src_ref=buffer.at[slot],
            dst_ref=buffer.at[slot],
            send_sem=send.at[k],
            recv_sem=recv.at[slot],
            device_id=(target, yz),
            device_id_type=MESH,
        )

    def offer(*where):
        for k in range(1, half):
            share(*where, gx, peer(k), k).start()
        share(*where, gx, partner, 0).start()

    def relay(*where):
        for k in range(1, half):
            share(*where, peer(k), peer(k), k).wait_recv()
            share(*where, peer(k), partner, half + k).start()

    def collect(*where):
        share(*where, partner, partner, 0).wait_recv()
        for k in range(1, half):
            share(*where, lax.rem(partner + 2 * k, n_gx), partner, half + k).wait_recv()

    def release(*where):
        share(*where, gx, partner, 0).wait_send()
        for k in range(1, half):
            share(*where, gx, peer(k), k).wait_send()
            share(*where, peer(k), partner, half + k).wait_send()

    maps = (gmap, map_send, map_recv)
    vecs = [(gvec.at[g], vec_send.at[g], vec_recv.at[g]) for g in range(groups)]
    offer(*maps)

    def local_forward(g):
        state = (jnp.zeros((nv, nz), F32), jnp.zeros((nv, nz), F32))
        for c in range(pieces):
            @pl.when(has_low)
            def _():
                halo(0, g, c).wait_recv()

            @pl.when(has_high)
            def _():
                halo(1, g, c).wait_recv()

            def forward(i, state):
                x = c * chunk + i
                last, first = state
                if g == 0:
                    derivative = 8.0 * res[x, 1] + low[g, x] - high[g, x]
                else:
                    derivative = low[g, x] + high[g, x] - 8.0 * res[x, 0]
                kind = cat[x][g : g + 1]
                weight = jnp.where(kind == 0, 1.0, jnp.where(kind == 2, 0.5, 0.0))
                force = weight * (res[x, g] + mul(held(g, 0), split(derivative)))
                driven = mul(get(vt, g, x), split(force))
                last = driven + mul(get(ft, g, x), split(last))
                first = first + mul(get(lam, g, x), split(driven))
                cs[g, x] = last
                return last, first

            state = loop(chunk, forward, state, chunk)
        gvec[g, gx, :nv] = state[0]
        gvec[g, gx, nv:] = state[1]

    def local_backward():
        for g in range(groups):
            into_state[g] = cs[g, cells - 1]

        def backward(i, carry):
            x = cells - 2 - i
            for g in range(groups):
                state = cs[g, x] + mul(get(bt, g, x), split(into_state[g]))
                into_state[g] = state
                cs[g, x] = state
            return carry

        lax.fori_loop(0, cells - 1, backward, 0)

    def finish(g):
        total = jnp.zeros((2 * nv, nz), F32)
        tail = jnp.zeros((nv, nz), F32)
        for j in range(n_gx):
            total = total + mul(get(wc, g, j), split(gvec[g, j, :nv]))
            tail = tail + mul(get(wl, g, j), split(gvec[g, j, nv:]))
        into[g, 0, :nv], into[g, 1, :nv] = split(total[:nv])
        into[g, 0, nv:], into[g, 1, nv:] = split(total[nv:] + tail)

        def fix(x, carry):
            value = cs[g, x] + mul(get(resp, g, x), (into[g, 0], into[g, 1]))
            out[x, g] = jnp.where(cat[x][g : g + 1] != 1, value, 0.0)
            return carry

        loop(cells, fix, 0, 4)

    local_forward(0)
    offer(*vecs[0])
    relay(*maps)
    collect(*maps)

    for g in range(groups):
        side[g] = jnp.zeros((nv, nv), F32)
        tall[g] = jnp.zeros((2 * nv, nv), F32)

    def suffix(j, carry):
        here = jnp.where(gx == j, 1.0, 0.0)
        for g in range(groups):
            e = split(side[g])
            put(wl, g, j, e)
            both = mul(e, split(gmap[j, g * nv : (g + 1) * nv]))
            side[g] = both[:, nv:] + here * unit
            hom[g, j] = both
        return carry

    loop(n_gx, suffix, 0)

    def prefix(i, carry):
        j = n_gx - 1 - i
        here = jnp.where(gx == j, 1.0, 0.0)
        maps_here = gmap[j, groups * nv :]
        for g in range(groups):
            xs = split(tall[g])
            put(wc, g, j, xs)
            nxt = mul(xs, split(maps_here[:, g * nv : (g + 1) * nv]))
            tall[g, :nv] = nxt[:nv] + here * unit
            tall[g, nv:] = nxt[nv:] + hom[g, j][:, :nv]
        return carry

    loop(n_gx, prefix, 0)

    relay(*vecs[0])
    for g in range(1, groups):
        local_forward(g)
        offer(*vecs[g])
    local_backward()
    for g in range(1, groups):
        relay(*vecs[g])
    for g in range(groups):
        collect(*vecs[g])
        finish(g)

    @pl.when(has_high)
    def _():
        for g in range(groups):
            for c in range(pieces):
                halo(0, g, c).wait_send()

    @pl.when(has_low)
    def _():
        for g in range(groups):
            for c in range(pieces):
                halo(1, g, c).wait_send()

    release(*maps)
    for g in range(groups):
        release(*vecs[g])


def per_device(n_gx, n_yz, residual, inverses, upwind, downwind, flux_y, kinds, volume_category):
    cells, groups, nv, nz = residual.shape
    chunk = next(c for c in (3, 4, 2, 1) if cells % c == 0)
    pieces = cells // chunk
    hbm = pl.BlockSpec(memory_space=pltpu.HBM)
    operands = (residual, inverses, upwind, downwind, flux_y, volume_category, kinds)
    square = pltpu.VMEM((groups, cells, 2, nv, nv), BF16)
    wide = pltpu.VMEM((groups, cells, nv, nz), F32)
    return pl.pallas_call(
        functools.partial(kernel, n_gx, n_yz, chunk),
        out_shape=jax.ShapeDtypeStruct(residual.shape, F32),
        in_specs=[hbm] * 7,
        out_specs=pl.BlockSpec(memory_space=pltpu.VMEM),
        scratch_shapes=[pltpu.VMEM(a.shape, a.dtype) for a in operands[:-1]]
        + [
            pltpu.SMEM(kinds.shape, kinds.dtype),
            pltpu.VMEM((2, cells, nv, nz), F32),
            wide,
            wide,
            pltpu.VMEM((groups, 3, 2, nv, nv), BF16),
            square,
            square,
            square,
            pltpu.VMEM((groups, max(cells, n_gx) + 1, nv, 2 * nv), F32),
            pltpu.VMEM((groups, cells + 1, nv, nv), F32),
            square,
            pltpu.VMEM((groups, cells, 2, nv, 2 * nv), BF16),
            wide,
            pltpu.VMEM((n_gx, (groups + 1) * nv, 2 * nv), F32),
            pltpu.VMEM((groups, n_gx, 2 * nv, nz), F32),
            pltpu.VMEM((groups, n_gx, 2, 2 * nv, nv), BF16),
            pltpu.VMEM((groups, n_gx, 2, nv, nv), BF16),
            pltpu.VMEM((groups, 2, 2 * nv, nz), BF16),
            pltpu.VMEM((groups, nv, nv), F32),
            pltpu.VMEM((groups, nv, 2 * nv), F32),
            pltpu.VMEM((groups, 2 * nv, nv), F32),
            pltpu.VMEM((groups, nv, nz), F32),
            pltpu.SemaphoreType.DMA((7,)),
            pltpu.SemaphoreType.DMA((2, groups, pieces)),
            pltpu.SemaphoreType.DMA((2, groups, pieces)),
            pltpu.SemaphoreType.DMA((n_gx,)),
            pltpu.SemaphoreType.DMA((n_gx,)),
            pltpu.SemaphoreType.DMA((groups, n_gx)),
            pltpu.SemaphoreType.DMA((groups, n_gx)),
        ],
        compiler_params=pltpu.CompilerParams(
            collective_id=0, has_side_effects=True, vmem_limit_bytes=48 * 1024 * 1024
        ),
    )(*(pltpu.with_memory_space_constraint(a, pltpu.HBM) for a in operands))


def solution(mesh):
    in_specs = (
        P("gx", "yz", None, None),
        P("gx", "yz", None, None),
        P(),
        P(),
        P(),
        P("yz"),
        P("gx", "yz", None),
    )
    out_specs = P("gx", "yz", None, None)
    return jax.shard_map(
        functools.partial(per_device, mesh.shape["gx"], mesh.shape["yz"]),
        mesh=mesh,
        in_specs=in_specs,
        out_specs=out_specs,
        check_vma=False,
    )
```
